512 devices in a mesh: table: 64 (over x, y, core), segment: 8 (over z).
Axes of the slice: x: 4, y: 8, z: 8, core: 2. Of those that a mesh axis runs over, the one named last changes fastest.
Arguments:
- hidden: bfloat16 [8, 16384, 1280], P('segment', 'table'), may hold values from -6 to 6
- owner: int32 [8, 16384, 8], P('segment', 'table'), may hold values from 0 to 63, all different within a row; in each aligned block of 256 rows (0 to 255, 256 to 511, ..., all dimensions but the last counted through in order) at most 64 rows name the same one
- slot: int32 [8, 16384, 8], P('segment', 'table'), may hold values from 0 to 127
- memory_table: bfloat16 [8, 8192, 640], P('segment', 'table'), may hold values from -6 to 6
- key_weight: bfloat16 [8, 640, 1280], P('segment'), may hold values from -0.25 to 0.25
- value_weight: bfloat16 [8, 640, 1280], P('segment'), may hold values from -0.25 to 0.25
- conv_weight: float32 [8, 4, 1280], P('segment'), may hold values from -3 to 3
Outputs:
- passed: bfloat16 [8, 16384, 1280], P('segment', 'table')
The draws below stay inside these ranges and needn't reach their ends.
Inputs may be any that keep to these rules, and one draw needn't show every extreme that they name: `owner`: A token's 8 heads name different shards; among the tokens of one device no shard is named by more than 64 lookups, a bound that some block reaches.
All inputs are finite; a program needn't handle non-finite values.
Results may differ from the reference program's by a relative error of at most 0.0047.
Values may be sent and summed in bfloat16 or wider, within the bound.
No kernel may reach another device: no remote copies, remote signals or barrier semaphores. Data moves between devices by JAX's collectives and lax.ppermute only.
A program may use at most 64 MiB of HBM per device.

```python
import math
import jax
import jax.numpy as jnp
import numpy as np
from jax import lax

D = 1280
DE = 640
HEADS = 8
KW = 4
CONV_DILATION = 3
TOK_DEV = 256
ROWS = 8192
SEQUENCE_TOKENS = 16384
ROWS_DEV = 128
MOST = 64
N_TABLE = 64
N_SEGMENT = 8


def with_ends(values, own_key, low, high):
    dims = values.shape
    place = [jax.random.randint(jax.random.fold_in(own_key, axis), (), 0, dims[axis]) for axis in range(len(dims))]
    values = values.at[tuple(place)].set(low)
    longest = dims.index(max(dims))
    place[longest] = (place[longest] + 1) % dims[longest]
    return values.at[tuple(place)].set(high)


def block_scale(own_key, shape, cuts, low, largest):
    def one(axis_at, shards_of):
        steps = jax.random.uniform(jax.random.fold_in(jax.random.fold_in(own_key, 6), axis_at), (shards_of,), jnp.float32, low / len(cuts), largest / len(cuts))
        return jnp.repeat(jnp.exp(steps), shape[axis_at] // shards_of).reshape((-1,) + (1,) * (len(shape) - axis_at - 1))

    level = one(*cuts[0])
    for cut in cuts[1:]:
        level = level * one(*cut)
    return level


def routed_block(own_key, own, number, rows, number_of, top, reach, skew):
    ranking = jax.random.permutation(own_key, number_of)
    heavy_load, ordinary = load_shares(number_of, rows * top, reach, skew, True), load_shares(number_of, rows * top, reach, skew, False)
    places = jnp.arange(number_of)

    def named(sizes, turn):
        used = int((sizes > 0).sum())
        fixed = max(1, used // 4)
        moved = fixed + (places - fixed + turn * (used - fixed)) % max(1, number_of - fixed)
        return jnp.zeros((number_of,), jnp.int32).at[ranking[jnp.where(places < fixed, places, moved)]].set(jnp.asarray(sizes, jnp.int32))

    sizes = jnp.where(number % 4 == 0, named(heavy_load, number // 4), named(ordinary, number - number // 4 - 1))
    mixed = jax.random.permutation(jax.random.fold_in(own, 3), number_of)
    giver, sink = mixed[0:number_of // 2 * 2:2], mixed[1:number_of // 2 * 2:2]
    room = jnp.minimum(sizes[giver] - 1, reach - sizes[sink]) // 2
    room = jnp.where((giver == ranking[0]) | (sink == ranking[0]) | (sizes[sink] == 0), 0, jnp.maximum(room, 0))
    moved = jax.random.randint(jax.random.fold_in(own, 4), (number_of // 2,), 0, 1 << 20) % (room + 1)
    sizes = sizes.at[giver].add(-moved).at[sink].add(moved)
    labels = jnp.searchsorted(jnp.cumsum(sizes), jnp.arange(rows * top), side="right").astype(jnp.int32)
    grid = labels.reshape(top, rows).T
    grid = grid[jax.random.permutation(jax.random.fold_in(own, 1), rows)]
    turn = jax.random.randint(jax.random.fold_in(own, 2), (rows, 1), 0, top)
    return jnp.take_along_axis(grid, (jnp.arange(top)[None, :] + turn) % top, axis=1)


def load_shares(count, total, bound, slope, full):
    weights = [(1 << 20) // math.isqrt(rank ** slope) + 1 for rank in range(1, count + 1)]
    largest = bound if full else min(bound, max(-(-total // count), total * weights[0] // sum(weights)))
    least = 1 if total - largest >= count - 1 else 0
    given, surplus = [largest] + [least] * (count - 1), total - largest - least * (count - 1)
    while surplus > 0:
        candidates = [i for i in range(1, count) if given[i] < largest] or [i for i in range(1, count) if given[i] < bound]
        pool, remaining = sum([weights[i] for i in candidates]), surplus
        for i in candidates:
            more = min(bound - given[i], max(1, remaining * weights[i] // pool), surplus)
            given[i] = given[i] + more
            surplus = surplus - more
    return np.array(given)


def centred(key, shape, width, most, cuts=(), dtype=jnp.bfloat16):
    values = jax.random.normal(key, shape, jnp.float32) * width
    if len(cuts) > 0:
        values = block_scale(key, shape, cuts, -0.22, 0.18) * values
    return jnp.clip(values, min=-most, max=most).astype(dtype)


def setup_inputs(seed: int = 0) -> dict:
    key_of = jax.random.split(jax.random.key(seed), 8)
    hidden = centred(key_of[0], (N_SEGMENT, SEQUENCE_TOKENS, D), 1.0, 6.0, ((0, 8), (1, 64)))
    owner_keys = jax.random.split(jax.random.fold_in(key_of[1], 1), N_SEGMENT * SEQUENCE_TOKENS // TOK_DEV)
    owner_turns = jax.random.permutation(jax.random.fold_in(key_of[1], 3), N_SEGMENT * SEQUENCE_TOKENS // TOK_DEV)
    owner = jax.vmap(lambda own, number: routed_block(jax.random.fold_in(key_of[1], 2), own, number, TOK_DEV, N_TABLE, HEADS, MOST, 2))(owner_keys, owner_turns).reshape((N_SEGMENT, SEQUENCE_TOKENS, HEADS))
    slot = with_ends(jax.random.randint(key_of[2], (N_SEGMENT, SEQUENCE_TOKENS, HEADS), 0, ROWS_DEV), jax.random.fold_in(key_of[2], 1), 0, ROWS_DEV - 1).astype(jnp.int32)
    memory_table = centred(key_of[3], (N_SEGMENT, ROWS, DE), 1.0, 6.0, ((0, 8), (1, 64)))
    key_weight = centred(key_of[4], (N_SEGMENT, DE, D), DE ** -0.5, 0.25, ((0, 8),))
    value_weight = centred(key_of[5], (N_SEGMENT, DE, D), DE ** -0.5, 0.25, ((0, 8),))
    conv_weight = centred(key_of[6], (N_SEGMENT, KW, D), 0.5, 3.0, ((0, 8),), jnp.float32)
    return dict(hidden=hidden, owner=owner, slot=slot, memory_table=memory_table, key_weight=key_weight, value_weight=value_weight, conv_weight=conv_weight)


def rms_scale(values):
    return values * lax.rsqrt(lax.optimization_barrier(jnp.mean(values * values, axis=-1, keepdims=True)) + 1e-06)

def one_section(operands):
    states, owners, slot_rows, table_rows, key_proj, value_proj, taps = operands
    global_ids = (owners * ROWS_DEV + slot_rows).astype(jnp.int32)
    memory = jnp.zeros((SEQUENCE_TOKENS, DE), jnp.float32)
    for head_index in range(HEADS):
        memory = memory + table_rows[global_ids[:, head_index]].astype(jnp.float32)
    packed = memory.astype(jnp.bfloat16)
    keys_out = jnp.dot(packed, key_proj, preferred_element_type=jnp.float32)
    values_out = jnp.dot(packed, value_proj, preferred_element_type=jnp.float32)
    states_float = states.astype(jnp.float32)
    affinity = lax.optimization_barrier(jnp.sum(rms_scale(states_float) * rms_scale(keys_out), axis=-1, keepdims=True)) / math.sqrt(D)
    gated_value = jax.nn.sigmoid(affinity) * values_out
    scaled_states = rms_scale(gated_value)
    convolved = jnp.zeros((SEQUENCE_TOKENS, D), jnp.float32)
    for kernel_tap_index in range(KW):
        lagged_states = jnp.pad(scaled_states, ((kernel_tap_index * CONV_DILATION, 0), (0, 0)))[:SEQUENCE_TOKENS]
        convolved = convolved + taps[kernel_tap_index] * lagged_states
    branch_out = jax.nn.silu(convolved) + gated_value
    return (states_float + branch_out).astype(jnp.bfloat16)

def reference(hidden, owner, slot, memory_table, key_weight, value_weight, conv_weight):
    result = lax.map(one_section, (hidden, owner, slot, memory_table, key_weight, value_weight, conv_weight))
    return jnp.roll(result, 1, axis=0)
```

```python
import math

import jax
import jax.numpy as jnp
from jax import lax
from jax.sharding import Mesh, PartitionSpec as P

CONV_DILATION = 3
NX, NY, NC = 4, 8, 2
HALO = 16
CHUNKS = 1
TABLE = ("x", "y", "core")


def rotated(value, axis, by):
    count = lax.axis_size(axis)
    return lax.ppermute(value, axis, [(i, (i + by) % count) for i in range(count)])


def rms_scale(values):
    return values * lax.rsqrt(jnp.mean(values * values, axis=-1, keepdims=True) + 1e-06)


def local(hidden, owner, slot, memory_table, key_weight, value_weight, conv_weight):
    states = hidden[0]
    table_local = memory_table[0]
    tok_rows, head_count = owner.shape[1:]
    features = states.shape[1]
    rows_dev, row_features = table_local.shape
    x, y, core = (lax.axis_index(name) for name in TABLE)
    first = (x == 0) & (y == 0) & (core == 0)

    blocks = {0: table_local}
    for step in (4, 3, 5, 2, 6, 1, 7):
        blocks[step] = rotated(table_local, "y", step)
    own_rows = jnp.concatenate([blocks[k] for k in range(NY)], axis=0)
    other_rows = rotated(own_rows, "core", 1)

    bf16 = jnp.bfloat16
    tail = jnp.concatenate(
        [
            states[tok_rows - HALO :],
            owner[0, tok_rows - HALO :].astype(bf16),
            slot[0, tok_rows - HALO :].astype(bf16),
            jnp.zeros((HALO, 128 - 2 * head_count), bf16),
        ],
        axis=1,
    )
    shards = NX * NY * NC
    head = lax.ppermute(tail, TABLE, [(i, i + 1) for i in range(shards - 1)])
    halo_owner = head[:, features : features + head_count].astype(jnp.int32)
    halo_slot = head[:, features + head_count : features + 2 * head_count].astype(jnp.int32)
    ext_states = jnp.concatenate([head[:, :features], states], axis=0)
    ext_owner = jnp.concatenate([halo_owner, owner[0]], axis=0).T
    ext_slot = jnp.concatenate([halo_slot, slot[0]], axis=0).T

    place = lax.broadcasted_iota(jnp.int32, (NX * NY * NC, 1), 0)
    to_x, far, swapped = place // (NY * NC), place // NC % NY, place % NC
    shard = to_x * (NY * NC) + ((y - far) % NY) * NC + (core ^ swapped)
    asked = jnp.full((shards, tok_rows + HALO), -1, jnp.int32)
    for h in range(head_count):
        asked = jnp.maximum(asked, jnp.where(ext_owner[h][None, :] == shard, ext_slot[h][None, :], -1))
    asked = lax.all_to_all(
        asked.reshape(NX, NY * NC, tok_rows + HALO), "x", split_axis=0, concat_axis=0, tiled=True
    )
    asked = asked.reshape(NX, NY, NC, tok_rows + HALO).transpose(0, 3, 2, 1)

    states_float = ext_states.astype(jnp.float32)
    scaled_hidden = rms_scale(states_float)
    chunk = tok_rows // CHUNKS
    out = []
    for c in range(CHUNKS):
        span = slice(c * chunk, c * chunk + chunk + HALO)
        rows = chunk + HALO
        mine = asked[:, span]
        lane = jnp.arange(rows_dev, dtype=jnp.int32)
        pick = (mine[..., None] == lane).astype(bf16).reshape(NX * rows, NC, NY * rows_dev)
        partial = jnp.dot(pick[:, 0], own_rows, preferred_element_type=jnp.float32) + jnp.dot(
            pick[:, 1], other_rows, preferred_element_type=jnp.float32
        )
        partial = lax.all_to_all(
            partial.astype(bf16).reshape(NX, rows, row_features), "x", split_axis=0, concat_axis=0, tiled=True
        )
        packed = jnp.sum(partial.astype(jnp.float32), axis=0).astype(bf16)
        keys_out = jnp.dot(packed, key_weight[0], preferred_element_type=jnp.float32)
        values_out = jnp.dot(packed, value_weight[0], preferred_element_type=jnp.float32)
        affinity = jnp.sum(
            scaled_hidden[span] * rms_scale(keys_out), axis=-1, keepdims=True
        ) / math.sqrt(features)
        gated = jax.nn.sigmoid(affinity) * values_out
        normed = rms_scale(gated)
        if c == 0:
            before = lax.broadcasted_iota(jnp.int32, (rows, 1), 0) < HALO
            normed = jnp.where(before & first, 0.0, normed)
        convolved = jnp.zeros((chunk, features), jnp.float32)
        for k in range(conv_weight.shape[1]):
            start = HALO - k * CONV_DILATION
            convolved = convolved + conv_weight[0, k] * normed[start : start + chunk]
        branch = jax.nn.silu(convolved) + gated[HALO:]
        result = (states_float[span][HALO:] + branch).astype(bf16)
        out.append(rotated(result, "segment", 1))
    return jnp.concatenate(out, axis=0)[None]


def solution(mesh):
    grid = Mesh(mesh.devices.reshape(NX, NY, NC, -1), TABLE + ("segment",))
    in_specs = (
        P("segment", TABLE, None),
        P("segment", TABLE, None),
        P("segment", TABLE, None),
        P("segment", TABLE, None),
        P("segment", None, None),
        P("segment", None, None),
        P("segment", None, None),
    )
    out_specs = P("segment", TABLE, None)
    return jax.shard_map(local, mesh=grid, in_specs=in_specs, out_specs=out_specs, check_vma=False)
```

```python
import math

import jax
import jax.numpy as jnp
from jax import lax
from jax.experimental import pallas as pl
from jax.experimental.pallas import tpu as pltpu
from jax.sharding import Mesh, PartitionSpec as P


CONV_DILATION = 3
NX, NY, NC = 4, 8, 2
HALO = 16
TABLE = ("x", "y", "core")


def rotated(value, axis, by):
    count = lax.axis_size(axis)
    return lax.ppermute(value, axis, [(i, (i + by) % count) for i in range(count)])


def rms_scale(values):
    return values * lax.rsqrt(jnp.mean(values * values, axis=-1, keepdims=True) + 1e-06)


def pick_kernel(x_ref, asked_ref, own_ref, other_ref, *, rows_dev):
    lane = lax.broadcasted_iota(jnp.int32, (asked_ref.shape[1], rows_dev), 1)
    for swapped, out_ref in ((0, own_ref), (1, other_ref)):
        for far in range(NY):
            column = swapped * NY + far
            hit = asked_ref[0, :, column : column + 1] == lane
            out_ref[0, :, far * rows_dev : (far + 1) * rows_dev] = hit.astype(jnp.float32).astype(jnp.bfloat16)


def pick_matrices(x, asked, rows_dev):
    groups, rows, columns = asked.shape
    shape = jax.ShapeDtypeStruct((groups, rows, NY * rows_dev), jnp.bfloat16)
    spec = pl.BlockSpec((1, rows, NY * rows_dev), lambda i, x_ref: (i, 0, 0))
    return pl.pallas_call(
        lambda *refs: pick_kernel(*refs, rows_dev=rows_dev),
        grid_spec=pltpu.PrefetchScalarGridSpec(
            num_scalar_prefetch=1,
            grid=(groups,),
            in_specs=[
                pl.BlockSpec((1, rows, columns), lambda i, x_ref: (lax.rem(x_ref[0] - i + groups, groups), 0, 0))
            ],
            out_specs=[spec, spec],
        ),
        out_shape=[shape, shape],
        name="pick_matrices",
    )(x.astype(jnp.int32).reshape(1), asked)


def local(hidden, owner, slot, memory_table, key_weight, value_weight, conv_weight):
    bf16 = jnp.bfloat16
    tok_rows, head_count = owner.shape[1:]
    features = hidden.shape[2]
    rows_dev, row_features = memory_table.shape[1:]
    x, y, core = (lax.axis_index(name) for name in TABLE)
    first = (x == 0) & (y == 0) & (core == 0)

    table = rotated(memory_table[0], "segment", 1)
    numbers = jnp.concatenate([owner[0].T, slot[0].T], axis=0)
    numbers = rotated(numbers, "segment", 1)
    tail = jnp.concatenate(
        [
            hidden[0, tok_rows - HALO :],
            owner[0, tok_rows - HALO :].astype(bf16),
            slot[0, tok_rows - HALO :].astype(bf16),
            jnp.zeros((HALO, 128 - 2 * head_count), bf16),
        ],
        axis=1,
    )
    shards = NX * NY * NC
    sections = lax.axis_size("segment")
    tail = lax.ppermute(
        tail,
        TABLE + ("segment",),
        [
            (i * sections + s, (i + 1) * sections + (s + 1) % sections)
            for i in range(shards - 1)
            for s in range(sections)
        ],
    )
    states = rotated(hidden[0], "segment", 1)
    weight_one = jnp.where(core == 0, key_weight[0], value_weight[0])
    weight_one = rotated(weight_one, "segment", 1)
    weight_two = rotated(weight_one, "core", 1)
    taps = rotated(conv_weight[0], "segment", 1)

    copies = jnp.broadcast_to(table[None], (NY, rows_dev, row_features))
    own_rows = lax.all_to_all(copies, "y", split_axis=0, concat_axis=0, tiled=True)
    own_rows = own_rows.reshape(NY * rows_dev, row_features)
    other_rows = rotated(own_rows, "core", 1)

    head_numbers = tail[:, features : features + 2 * head_count].astype(jnp.int32).T
    numbers = jnp.concatenate([head_numbers, numbers], axis=1)
    place = lax.broadcasted_iota(jnp.int32, (shards, 1), 0)
    ahead, swapped, far = place // (NY * NC), place // NY % NC, place % NY
    shard = (x + ahead) % NX * (NY * NC) + far * NC + (core ^ swapped)
    asked = jnp.full((shards, tok_rows + HALO), -1, jnp.int32)
    for h in range(head_count):
        asked = jnp.maximum(
            asked, jnp.where(numbers[h][None, :] == shard, numbers[head_count + h][None, :], -1)
        )
    asked = asked.reshape(NX, NY * NC, tok_rows + HALO)
    received = [asked[0]]
    for ahead in range(1, NX):
        received.append(rotated(asked[ahead], "x", ahead))
    asked = jnp.stack(received).transpose(0, 2, 1)
    pick_own, pick_other = pick_matrices(x, asked, rows_dev)

    rows = tok_rows + HALO
    other_part = jnp.dot(pick_other.reshape(NX * rows, -1), other_rows, preferred_element_type=jnp.float32)
    own_part = jnp.dot(pick_own.reshape(NX * rows, -1), own_rows, preferred_element_type=jnp.float32)
    partial = (other_part + own_part).astype(bf16).reshape(NX, rows, row_features)
    partial = lax.all_to_all(partial, "x", split_axis=0, concat_axis=0, tiled=True)
    packed = jnp.sum(partial.astype(jnp.float32), axis=0).astype(bf16)

    states_float = jnp.concatenate([tail[:, :features], states], axis=0).astype(jnp.float32)
    one = jnp.dot(packed, weight_one, preferred_element_type=jnp.float32)
    two = jnp.dot(packed, weight_two, preferred_element_type=jnp.float32)
    keys_out = jnp.where(core == 0, one, two)
    values_out = jnp.where(core == 0, two, one)
    affinity = jnp.sum(rms_scale(states_float) * rms_scale(keys_out), axis=-1, keepdims=True) / math.sqrt(features)
    gated = jax.nn.sigmoid(affinity) * values_out
    normed = rms_scale(gated)
    before = lax.broadcasted_iota(jnp.int32, (rows, 1), 0) < HALO
    normed = jnp.where(before & first, 0.0, normed)
    convolved = jnp.zeros((tok_rows, features), jnp.float32)
    for k in range(taps.shape[0]):
        start = HALO - k * CONV_DILATION
        convolved = convolved + taps[k] * normed[start : start + tok_rows]
    branch = jax.nn.silu(convolved) + gated[HALO:]
    return (states_float[HALO:] + branch).astype(bf16)[None]


def solution(mesh):
    grid = Mesh(mesh.devices.reshape(NX, NY, NC, -1), TABLE + ("segment",))
    in_specs = (
        P("segment", TABLE, None),
        P("segment", TABLE, None),
        P("segment", TABLE, None),
        P("segment", TABLE, None),
        P("segment", None, None),
        P("segment", None, None),
        P("segment", None, None),
    )
    out_specs = P("segment", TABLE, None)

    return jax.shard_map(local, mesh=grid, in_specs=in_specs, out_specs=out_specs, check_vma=False)
```

```python
import math

import jax
import jax.numpy as jnp
import numpy as np
from jax import lax
from jax.experimental import pallas as pl
from jax.experimental.pallas import tpu as pltpu
from jax.sharding import Mesh, PartitionSpec as P


CONV_DILATION = 3
NX, NY, NC = 4, 8, 2
HALO = 16
CHUNKS = 2
TABLE = ("x", "y", "core")
OFFSETS = (0, 1, -1, -2, 2, 3, -3, -4)


VMEM = pl.BlockSpec(memory_space=pltpu.VMEM)
SMEM = pl.BlockSpec(memory_space=pltpu.SMEM)


def rotated(value, axis, by):
    count = lax.axis_size(axis)
    return lax.ppermute(value, axis, [(i, (i + by) % count) for i in range(count)])


def exchanged(value, sign):
    pairs = []
    for y in range(NY):
        for core in range(NC):
            step = sign if (y + core) % 2 == 0 else -sign
            pairs.append((y * NC + core, (y + step) % NY * NC + core))
    return lax.ppermute(value, ("y", "core"), pairs)


def call(body, out_shape, *operands, smem=0):
    return pl.pallas_call(
        body, in_specs=[SMEM] * smem + [VMEM] * (len(operands) - smem), out_specs=VMEM, out_shape=out_shape
    )(*operands)


def stacked(*pieces):
    def body(*refs):
        at = 0
        for ref in refs[:-1]:
            refs[-1][at : at + ref.shape[0]] = ref[...]
            at += ref.shape[0]

    rows = sum(piece.shape[0] for piece in pieces)
    return call(body, jax.ShapeDtypeStruct((rows, pieces[0].shape[1]), pieces[0].dtype), *pieces)


def picked(asked, first_column, pieces, rows_dev):
    lane = lax.broadcasted_iota(jnp.int32, (asked.shape[0], rows_dev), 1)
    total, column = None, first_column
    for piece in pieces:
        hits = []
        for _ in range(piece.shape[0] // rows_dev):
            hit = asked[:, column : column + 1] == lane
            hits.append(hit.astype(jnp.float32).astype(jnp.bfloat16))
            column += 1
        part = jnp.dot(jnp.concatenate(hits, axis=1), piece[...], preferred_element_type=jnp.float32)
        total = part if total is None else total + part
    return total


def pick_own(x, asked, pieces, rows_dev):
    groups, rows, _ = asked.shape

    def body(x_ref, asked_ref, *refs):
        for group in range(groups):
            source = lax.rem(x_ref[0] - group + groups, groups)
            refs[-1][group] = picked(asked_ref[source], 0, refs[:-1], rows_dev)

    shape = jax.ShapeDtypeStruct((groups, rows, pieces[0].shape[1]), jnp.float32)
    return call(body, shape, x, asked, *pieces, smem=1)


def pick_other(x, asked, own, pieces, rows_dev, start, rows):
    groups = asked.shape[0]

    def body(x_ref, asked_ref, own_ref, *refs):
        for group in range(groups):
            source = lax.rem(x_ref[0] - group + groups, groups)
            total = picked(asked_ref[source, start : start + rows], NY, refs[:-1], rows_dev)
            refs[-1][group] = (own_ref[group, start : start + rows] + total).astype(jnp.bfloat16)

    shape = jax.ShapeDtypeStruct((groups, rows, own.shape[2]), jnp.bfloat16)
    return call(body, shape, x, asked, own, *pieces, smem=1)


def dense(keep, sums, tail, hidden, key_weight, value_weight, taps, start, chunk):
    features = hidden.shape[1]
    rows = chunk + HALO

    def body(keep_ref, sums_ref, tail_ref, hidden_ref, key_ref, value_ref, taps_ref, out_ref, normed_ref):
        total = sums_ref[0].astype(jnp.float32)
        for group in range(1, sums_ref.shape[0]):
            total = total + sums_ref[group].astype(jnp.float32)
        packed = total.astype(jnp.bfloat16)
        if start == 0:
            states = jnp.concatenate([tail_ref[:, :features], hidden_ref[:chunk]], axis=0)
        else:
            states = hidden_ref[start - HALO : start + chunk]
        states = states.astype(jnp.float32)
        keys = jnp.dot(packed, key_ref[...], preferred_element_type=jnp.float32)
        mean_states = jnp.mean(states * states, axis=-1, keepdims=True)
        mean_keys = jnp.mean(keys * keys, axis=-1, keepdims=True)
        affinity = jnp.sum(states * keys, axis=-1, keepdims=True)
        affinity = affinity * lax.rsqrt(mean_states + 1e-06) * lax.rsqrt(mean_keys + 1e-06) / math.sqrt(features)
        values = jnp.dot(packed, value_ref[...], preferred_element_type=jnp.float32)
        gated = jax.nn.sigmoid(affinity) * values
        scale = lax.rsqrt(jnp.mean(gated * gated, axis=-1, keepdims=True) + 1e-06)
        normed_ref[...] = gated * scale
        if start == 0:
            normed_ref[:HALO] = jnp.where(keep_ref[0] > 0, normed_ref[:HALO], 0.0)
        convolved = taps_ref[0:1] * normed_ref[HALO:]
        for k in range(1, taps_ref.shape[0]):
            at = HALO - k * CONV_DILATION
            convolved = convolved + taps_ref[k : k + 1] * normed_ref[at : at + chunk]
        branch = convolved * jax.nn.sigmoid(convolved) + gated[HALO:]
        out_ref[...] = (states[HALO:] + branch).astype(jnp.bfloat16)

    return pl.pallas_call(
        body,
        in_specs=[SMEM] + [VMEM] * 6,
        out_specs=VMEM,
        out_shape=jax.ShapeDtypeStruct((chunk, features), jnp.bfloat16),
        scratch_shapes=[pltpu.VMEM((rows, features), jnp.float32)],
        name="dense",
    )(keep, sums, tail, hidden, key_weight, value_weight, taps)


def local(hidden, owner, slot, memory_table, key_weight, value_weight, conv_weight):
    bf16 = jnp.bfloat16
    tok_rows, head_count = owner.shape[1:]
    features = hidden.shape[2]
    rows_dev = memory_table.shape[1]
    x, y, core = (lax.axis_index(name) for name in TABLE)
    keep = ((x > 0) | (y > 0) | (core > 0)).astype(jnp.int32).reshape(1)
    place_x = x.astype(jnp.int32).reshape(1)
    shards = NX * NY * NC

    near = exchanged(memory_table[0], 1)
    tail = jnp.concatenate(
        [
            hidden[0, tok_rows - HALO :],
            owner[0, tok_rows - HALO :].astype(bf16),
            slot[0, tok_rows - HALO :].astype(bf16),
            jnp.zeros((HALO, 128 - 2 * head_count), bf16),
        ],
        axis=1,
    )
    tail = lax.ppermute(tail, TABLE, [(i, i + 1) for i in range(shards - 1)])
    pieces = [stacked(memory_table[0], near)]
    for step in (2, 3, 4):
        pieces.append(exchanged(pieces[-1], -1 if step % 2 == 0 else 1))
    early = stacked(*pieces[:3])
    early = rotated(early, "core", 1)
    late = rotated(pieces[3], "core", 1)

    head_numbers = tail[:, features : features + 2 * head_count].astype(jnp.int32).T
    numbers = jnp.concatenate([head_numbers, jnp.concatenate([owner[0].T, slot[0].T], axis=0)], axis=1)
    place = np.arange(shards)
    ahead, swapped, far = place // (NY * NC), place // NY % NC, place % NY
    steps = np.asarray(OFFSETS)[far] * np.where(swapped == 0, 1, -1)
    ahead, swapped, steps = (jnp.asarray(v, jnp.int32)[:, None] for v in (ahead, swapped, steps))
    towards = jnp.where((y + core) % 2 == 0, 1, -1)
    shard = (x + ahead) % NX * (NY * NC) + (y + towards * steps + NY) % NY * NC + (core ^ swapped)
    asked = jnp.full((shards, tok_rows + HALO), -1, jnp.int32)
    for h in range(head_count):
        asked = jnp.maximum(
            asked, jnp.where(numbers[h][None, :] == shard, numbers[head_count + h][None, :], -1)
        )
    asked = asked.reshape(NX, NY * NC, tok_rows + HALO)
    received = [asked[0]]
    for ahead in range(1, NX):
        received.append(rotated(asked[ahead], "x", ahead))
    asked = jnp.stack(received).transpose(0, 2, 1)

    own = pick_own(place_x, asked, pieces, rows_dev)
    chunk = tok_rows // CHUNKS
    out = []
    for c in range(CHUNKS):
        sums = pick_other(place_x, asked, own, [early, late], rows_dev, c * chunk, chunk + HALO)
        sums = lax.all_to_all(sums, "x", split_axis=0, concat_axis=0, tiled=True)
        result = dense(keep, sums, tail, hidden[0], key_weight[0], value_weight[0], conv_weight[0], c * chunk, chunk)
        out.append(rotated(result, "segment", 1))
    return jnp.concatenate(out, axis=0)[None]


def solution(mesh):
    grid = Mesh(mesh.devices.reshape(NX, NY, NC, -1), TABLE + ("segment",))
    in_specs = (
        P("segment", TABLE, None),
        P("segment", TABLE, None),
        P("segment", TABLE, None),
        P("segment", TABLE, None),
        P("segment", None, None),
        P("segment", None, None),
        P("segment", None, None),
    )
    out_specs = P("segment", TABLE, None)

    return jax.shard_map(local, mesh=grid, in_specs=in_specs, out_specs=out_specs, check_vma=False)
```

```python
import math

import jax
import jax.numpy as jnp
from jax import lax
from jax.experimental import pallas as pl
from jax.experimental.pallas import tpu as pltpu
from jax.sharding import Mesh, PartitionSpec as P


CONV_DILATION = 3
NX, NY, NC = 4, 8, 2
HALO = 16
TABLE = ("x", "y", "core")


def rotated(value, axis, by):
    count = lax.axis_size(axis)
    return lax.ppermute(value, axis, [(i, (i + by) % count) for i in range(count)])


VMEM = pl.BlockSpec(memory_space=pltpu.VMEM)
SMEM = pl.BlockSpec(memory_space=pltpu.SMEM)


def pick_matrices(x, asked, rows_dev):
    groups, rows, _ = asked.shape

    def body(x_ref, asked_ref, own_ref, other_ref):
        lane = lax.broadcasted_iota(jnp.int32, (rows, rows_dev), 1)
        for group in range(groups):
            source = lax.rem(x_ref[0] - group + groups, groups)
            for swapped, out_ref in ((0, own_ref), (1, other_ref)):
                for far in range(NY):
                    column = swapped * NY + far
                    hit = asked_ref[source, :, column : column + 1] == lane
                    hit = hit.astype(jnp.float32).astype(jnp.bfloat16)
                    out_ref[group, :, far * rows_dev : (far + 1) * rows_dev] = hit

    shape = jax.ShapeDtypeStruct((groups, rows, NY * rows_dev), jnp.bfloat16)
    return pl.pallas_call(
        body,
        in_specs=[SMEM, VMEM],
        out_specs=[VMEM, VMEM],
        out_shape=[shape, shape],
        name="pick_matrices",
    )(x, asked)


def dot_own(pick, table_rows):
    groups, rows, _ = pick.shape

    def body(pick_ref, rows_ref, out_ref):
        for group in range(groups):
            out_ref[group] = jnp.dot(pick_ref[group], rows_ref[...], preferred_element_type=jnp.float32)

    return pl.pallas_call(
        body,
        in_specs=[VMEM, VMEM],
        out_specs=VMEM,
        out_shape=jax.ShapeDtypeStruct((groups, rows, table_rows.shape[1]), jnp.float32),
        name="dot_own",
    )(pick, table_rows)


def dot_other(pick, table_rows, own):
    def body(pick_ref, rows_ref, own_ref, out_ref):
        for group in range(own.shape[0]):
            total = jnp.dot(pick_ref[group], rows_ref[...], preferred_element_type=jnp.float32)
            out_ref[group] = (own_ref[group] + total).astype(jnp.bfloat16)

    return pl.pallas_call(
        body,
        in_specs=[VMEM, VMEM, VMEM],
        out_specs=VMEM,
        out_shape=jax.ShapeDtypeStruct(own.shape, jnp.bfloat16),
        name="dot_other",
    )(pick, table_rows, own)


def dense(place, sums, tail, hidden, weight_one, weight_two, taps):
    chunk, features = hidden.shape
    rows = chunk + HALO

    def body(place_ref, sums_ref, tail_ref, hidden_ref, one_ref, two_ref, taps_ref, out_ref, product_ref, normed_ref):
        total = sums_ref[0].astype(jnp.float32)
        for group in range(1, sums_ref.shape[0]):
            total = total + sums_ref[group].astype(jnp.float32)
        packed = total.astype(jnp.bfloat16)
        core = place_ref[1]
        product_ref[core] = jnp.dot(packed, one_ref[...], preferred_element_type=jnp.float32)
        product_ref[1 - core] = jnp.dot(packed, two_ref[...], preferred_element_type=jnp.float32)
        states = jnp.concatenate([tail_ref[:, :features], hidden_ref[...]], axis=0).astype(jnp.float32)
        keys = product_ref[0]
        mean_states = jnp.mean(states * states, axis=-1, keepdims=True)
        mean_keys = jnp.mean(keys * keys, axis=-1, keepdims=True)
        affinity = jnp.sum(states * keys, axis=-1, keepdims=True)
        affinity = affinity * lax.rsqrt(mean_states + 1e-06) * lax.rsqrt(mean_keys + 1e-06) / math.sqrt(features)
        gated = jax.nn.sigmoid(affinity) * product_ref[1]
        product_ref[1] = gated
        scale = lax.rsqrt(jnp.mean(gated * gated, axis=-1, keepdims=True) + 1e-06)
        normed_ref[...] = gated * scale
        normed_ref[:HALO] = jnp.where(place_ref[0] > 0, normed_ref[:HALO], 0.0)
        convolved = taps_ref[0:1] * normed_ref[HALO:]
        for k in range(1, taps_ref.shape[0]):
            at = HALO - k * CONV_DILATION
            convolved = convolved + taps_ref[k : k + 1] * normed_ref[at : at + chunk]
        branch = convolved * jax.nn.sigmoid(convolved) + product_ref[1, HALO:]
        out_ref[...] = (hidden_ref[...].astype(jnp.float32) + branch).astype(jnp.bfloat16)

    return pl.pallas_call(
        body,
        in_specs=[SMEM] + [VMEM] * 6,
        out_specs=VMEM,
        out_shape=jax.ShapeDtypeStruct((chunk, features), jnp.bfloat16),
        scratch_shapes=[
            pltpu.VMEM((2, rows, features), jnp.float32),
            pltpu.VMEM((rows, features), jnp.float32),
        ],
        name="dense",
    )(place, sums, tail, hidden, weight_one, weight_two, taps)


def local(hidden, owner, slot, memory_table, key_weight, value_weight, conv_weight):
    bf16 = jnp.bfloat16
    tok_rows, head_count = owner.shape[1:]
    features = hidden.shape[2]
    rows_dev, row_features = memory_table.shape[1:]
    x, y, core = (lax.axis_index(name) for name in TABLE)

    table = rotated(memory_table[0], "segment", 1)
    numbers = jnp.concatenate([owner[0].T, slot[0].T], axis=0)
    numbers = rotated(numbers, "segment", 1)
    tail = jnp.concatenate(
        [
            hidden[0, tok_rows - HALO :],
            owner[0, tok_rows - HALO :].astype(bf16),
            slot[0, tok_rows - HALO :].astype(bf16),
            jnp.zeros((HALO, 128 - 2 * head_count), bf16),
        ],
        axis=1,
    )
    shards = NX * NY * NC
    sections = lax.axis_size("segment")
    tail = lax.ppermute(
        tail,
        TABLE + ("segment",),
        [
            (i * sections + s, (i + 1) * sections + (s + 1) % sections)
            for i in range(shards - 1)
            for s in range(sections)
        ],
    )
    states = rotated(hidden[0], "segment", 1)
    weight_one = jnp.where(core == 0, key_weight[0], value_weight[0])
    weight_one = rotated(weight_one, "segment", 1)
    weight_two = rotated(weight_one, "core", 1)
    taps = rotated(conv_weight[0], "segment", 1)

    copies = jnp.broadcast_to(table[None], (NY, rows_dev, row_features))
    own_rows = lax.all_to_all(copies, "y", split_axis=0, concat_axis=0, tiled=True)
    own_rows = own_rows.reshape(NY * rows_dev, row_features)
    other_rows = rotated(own_rows, "core", 1)

    head_numbers = tail[:, features : features + 2 * head_count].astype(jnp.int32).T
    numbers = jnp.concatenate([head_numbers, numbers], axis=1)
    place = lax.broadcasted_iota(jnp.int32, (shards, 1), 0)
    ahead, swapped, far = place // (NY * NC), place // NY % NC, place % NY
    shard = (x + ahead) % NX * (NY * NC) + far * NC + (core ^ swapped)
    asked = jnp.full((shards, tok_rows + HALO), -1, jnp.int32)
    for h in range(head_count):
        asked = jnp.maximum(
            asked, jnp.where(numbers[h][None, :] == shard, numbers[head_count + h][None, :], -1)
        )
    asked = asked.reshape(NX, NY * NC, tok_rows + HALO)
    received = [asked[0]]
    for ahead in range(1, NX):
        received.append(rotated(asked[ahead], "x", ahead))
    asked = jnp.stack(received).transpose(0, 2, 1)
    pick_own, pick_other = pick_matrices(x.astype(jnp.int32).reshape(1), asked, rows_dev)

    own_part = dot_own(pick_own, own_rows)
    sums = dot_other(pick_other, other_rows, own_part)
    sums = lax.all_to_all(sums, "x", split_axis=0, concat_axis=0, tiled=True)
    later = (x > 0) | (y > 0) | (core > 0)
    place = jnp.stack([later.astype(jnp.int32), core.astype(jnp.int32)])
    return dense(place, sums, tail, states, weight_one, weight_two, taps)[None]


def solution(mesh):
    grid = Mesh(mesh.devices.reshape(NX, NY, NC, -1), TABLE + ("segment",))
    in_specs = (
        P("segment", TABLE, None),
        P("segment", TABLE, None),
        P("segment", TABLE, None),
        P("segment", TABLE, None),
        P("segment", None, None),
        P("segment", None, None),
        P("segment", None, None),
    )
    out_specs = P("segment", TABLE, None)

    return jax.shard_map(local, mesh=grid, in_specs=in_specs, out_specs=out_specs, check_vma=False)
```

```python
import math

import jax
import jax.numpy as jnp
from jax import lax
from jax.experimental import pallas as pl
from jax.experimental.pallas import tpu as pltpu
from jax.sharding import Mesh, PartitionSpec as P


CONV_DILATION = 3
NX, NY, NC = 4, 8, 2
HALO = 16
TABLE = ("x", "y", "core")


def rotated(value, axis, by):
    count = lax.axis_size(axis)
    return lax.ppermute(value, axis, [(i, (i + by) % count) for i in range(count)])


VMEM = pl.BlockSpec(memory_space=pltpu.VMEM)
SMEM = pl.BlockSpec(memory_space=pltpu.SMEM)


def pick_matrices(asked, rows_dev):
    groups, rows, _ = asked.shape

    def body(asked_ref, own_ref, other_ref):
        lane = lax.broadcasted_iota(jnp.int32, (rows, rows_dev), 1)
        for group in range(groups):
            for swapped, out_ref in ((0, own_ref), (1, other_ref)):
                for far in range(NY):
                    column = swapped * NY + far
                    hit = asked_ref[group, :, column : column + 1] == lane
                    hit = hit.astype(jnp.float32).astype(jnp.bfloat16)
                    out_ref[group, :, far * rows_dev : (far + 1) * rows_dev] = hit

    shape = jax.ShapeDtypeStruct((groups, rows, NY * rows_dev), jnp.bfloat16)
    return pl.pallas_call(
        body,
        in_specs=[VMEM],
        out_specs=[VMEM, VMEM],
        out_shape=[shape, shape],
        name="pick_matrices",
    )(asked)


def dense(place, own, sums, tail, hidden, weight_one, weight_two, taps):
    chunk, features = hidden.shape
    rows = chunk + HALO

    def body(place_ref, own_ref, *refs):
        sums_refs, refs = refs[: len(sums)], refs[len(sums) :]
        tail_ref, hidden_ref, one_ref, two_ref, taps_ref, out_ref, product_ref, normed_ref = refs
        total = own_ref[...]
        for sums_ref in sums_refs:
            total = total + sums_ref[...].astype(jnp.float32)
        packed = total.astype(jnp.bfloat16)
        core = place_ref[1]
        product_ref[core] = jnp.dot(packed, one_ref[...], preferred_element_type=jnp.float32)
        product_ref[1 - core] = jnp.dot(packed, two_ref[...], preferred_element_type=jnp.float32)
        states = jnp.concatenate([tail_ref[:, :features], hidden_ref[...]], axis=0).astype(jnp.float32)
        keys = product_ref[0]
        mean_states = jnp.mean(states * states, axis=-1, keepdims=True)
        mean_keys = jnp.mean(keys * keys, axis=-1, keepdims=True)
        affinity = jnp.sum(states * keys, axis=-1, keepdims=True)
        affinity = affinity * lax.rsqrt(mean_states + 1e-06) * lax.rsqrt(mean_keys + 1e-06) / math.sqrt(features)
        gated = jax.nn.sigmoid(affinity) * product_ref[1]
        product_ref[1] = gated
        scale = lax.rsqrt(jnp.mean(gated * gated, axis=-1, keepdims=True) + 1e-06)
        normed_ref[...] = gated * scale
        normed_ref[:HALO] = jnp.where(place_ref[0] > 0, normed_ref[:HALO], 0.0)
        convolved = taps_ref[0:1] * normed_ref[HALO:]
        for k in range(1, taps_ref.shape[0]):
            at = HALO - k * CONV_DILATION
            convolved = convolved + taps_ref[k : k + 1] * normed_ref[at : at + chunk]
        branch = convolved * jax.nn.sigmoid(convolved) + product_ref[1, HALO:]
        out_ref[...] = (hidden_ref[...].astype(jnp.float32) + branch).astype(jnp.bfloat16)

    return pl.pallas_call(
        body,
        in_specs=[SMEM] + [VMEM] * (6 + len(sums)),
        out_specs=VMEM,
        out_shape=jax.ShapeDtypeStruct((chunk, features), jnp.bfloat16),
        scratch_shapes=[
            pltpu.VMEM((2, rows, features), jnp.float32),
            pltpu.VMEM((rows, features), jnp.float32),
        ],
        name="dense",
    )(place, own, *sums, tail, hidden, weight_one, weight_two, taps)


def local(hidden, owner, slot, memory_table, key_weight, value_weight, conv_weight):
    bf16 = jnp.bfloat16
    tok_rows, head_count = owner.shape[1:]
    features = hidden.shape[2]
    rows_dev, row_features = memory_table.shape[1:]
    x, y, core = (lax.axis_index(name) for name in TABLE)

    table = rotated(memory_table[0], "segment", 1)
    numbers = jnp.concatenate([owner[0].T, slot[0].T], axis=0)
    numbers = rotated(numbers, "segment", 1)
    tail = jnp.concatenate(
        [
            hidden[0, tok_rows - HALO :],
            owner[0, tok_rows - HALO :].astype(bf16),
            slot[0, tok_rows - HALO :].astype(bf16),
            jnp.zeros((HALO, 128 - 2 * head_count), bf16),
        ],
        axis=1,
    )
    shards = NX * NY * NC
    sections = lax.axis_size("segment")
    tail = lax.ppermute(
        tail,
        TABLE + ("segment",),
        [
            (i * sections + s, (i + 1) * sections + (s + 1) % sections)
            for i in range(shards - 1)
            for s in range(sections)
        ],
    )
    states = rotated(hidden[0], "segment", 1)
    weight_one = jnp.where(core == 0, key_weight[0], value_weight[0])
    weight_one = rotated(weight_one, "segment", 1)
    weight_two = rotated(weight_one, "core", 1)
    taps = rotated(conv_weight[0], "segment", 1)

    copies = jnp.broadcast_to(table[None], (NY, rows_dev, row_features))
    own_rows = lax.all_to_all(copies, "y", split_axis=0, concat_axis=0, tiled=True)
    own_rows = own_rows.reshape(NY * rows_dev, row_features)
    other_rows = rotated(own_rows, "core", 1)

    head_numbers = tail[:, features : features + 2 * head_count].astype(jnp.int32).T
    numbers = jnp.concatenate([head_numbers, numbers], axis=1)
    place = lax.broadcasted_iota(jnp.int32, (shards, 1), 0)
    ahead, swapped, far = place // (NY * NC), place // NY % NC, place % NY
    shard = (x + ahead) % NX * (NY * NC) + far * NC + (core ^ swapped)
    asked = jnp.full((shards, tok_rows + HALO), -1, jnp.int32)
    for h in range(head_count):
        asked = jnp.maximum(
            asked, jnp.where(numbers[h][None, :] == shard, numbers[head_count + h][None, :], -1)
        )
    asked = asked.reshape(NX, NY * NC, tok_rows + HALO)
    received = [asked[0]]
    for ahead in range(1, NX):
        received.append(rotated(asked[ahead], "x", ahead))
    asked = jnp.stack(received).transpose(0, 2, 1)
    pick_own, pick_other = pick_matrices(asked, rows_dev)

    rows = tok_rows + HALO
    own_part = jnp.dot(pick_own.reshape(NX * rows, -1), own_rows, preferred_element_type=jnp.float32)
    own_part = own_part.reshape(NX, rows, -1)
    sums = []
    for back in (2, 1, 3, 0):
        part = own_part[back] + jnp.dot(pick_other[back], other_rows, preferred_element_type=jnp.float32)
        if back > 0:
            sums.append(rotated(part.astype(bf16), "x", -back))
    later = (x > 0) | (y > 0) | (core > 0)
    place = jnp.stack([later.astype(jnp.int32), core.astype(jnp.int32)])
    return dense(place, part, sums, tail, states, weight_one, weight_two, taps)[None]


def solution(mesh):
    grid = Mesh(mesh.devices.reshape(NX, NY, NC, -1), TABLE + ("segment",))
    in_specs = (
        P("segment", TABLE, None),
        P("segment", TABLE, None),
        P("segment", TABLE, None),
        P("segment", TABLE, None),
        P("segment", None, None),
        P("segment", None, None),
        P("segment", None, None),
    )
    out_specs = P("segment", TABLE, None)

    return jax.shard_map(local, mesh=grid, in_specs=in_specs, out_specs=out_specs, check_vma=False)
```

```python
import math

import jax
import jax.numpy as jnp
from jax import lax
from jax.experimental import pallas as pl
from jax.experimental.pallas import tpu as pltpu
from jax.sharding import Mesh, PartitionSpec as P


CONV_DILATION = 3
NX, NY, NC = 4, 8, 2
HALO = 16
TABLE = ("x", "y", "core")


def rotated(value, axis, by):
    count = lax.axis_size(axis)
    return lax.ppermute(value, axis, [(i, (i + by) % count) for i in range(count)])


VMEM = pl.BlockSpec(memory_space=pltpu.VMEM)
SMEM = pl.BlockSpec(memory_space=pltpu.SMEM)


def pick_matrices(asked, rows_dev):
    groups, rows, _ = asked.shape

    def body(asked_ref, own_ref, other_ref):
        lane = lax.broadcasted_iota(jnp.int32, (rows, rows_dev), 1)
        for group in range(groups):
            for swapped, out_ref in ((0, own_ref), (1, other_ref)):
                for far in range(NY):
                    column = swapped * NY + far
                    hit = asked_ref[group, :, column : column + 1] == lane
                    hit = hit.astype(jnp.float32).astype(jnp.bfloat16)
                    out_ref[group, :, far * rows_dev : (far + 1) * rows_dev] = hit

    shape = jax.ShapeDtypeStruct((groups, rows, NY * rows_dev), jnp.bfloat16)
    return pl.pallas_call(
        body,
        in_specs=[VMEM],
        out_specs=[VMEM, VMEM],
        out_shape=[shape, shape],
        name="pick_matrices",
    )(asked)


ANY = pl.BlockSpec(memory_space=pl.ANY)


def edge_packet(hidden, owners, slots):
    heads, tok_rows = owners.shape
    features = hidden.shape[1]

    def body(hidden_ref, owners_ref, slots_ref, numbers_ref, tail_ref):
        numbers_ref[:heads] = owners_ref[...]
        numbers_ref[heads:] = slots_ref[...]
        tail_ref[:HALO] = hidden_ref[...]
        last = numbers_ref[:, tok_rows - 128 :].astype(jnp.float32)
        tail_ref[HALO:, :128] = last.astype(jnp.bfloat16)
        tail_ref[HALO:, 128:] = jnp.zeros((2 * heads, features - 128), jnp.bfloat16)

    return pl.pallas_call(
        body,
        grid=(1,),
        in_specs=[
            pl.BlockSpec((HALO, features), lambda i: (tok_rows // HALO - 1, 0)),
            pl.BlockSpec((heads, tok_rows), lambda i: (0, 0)),
            pl.BlockSpec((heads, tok_rows), lambda i: (0, 0)),
        ],
        out_specs=[
            pl.BlockSpec((2 * heads, tok_rows), lambda i: (0, 0)),
            pl.BlockSpec((HALO + 2 * heads, features), lambda i: (0, 0)),
        ],
        out_shape=[
            jax.ShapeDtypeStruct((2 * heads, tok_rows), jnp.int32),
            jax.ShapeDtypeStruct((HALO + 2 * heads, features), jnp.bfloat16),
        ],
        name="edge_packet",
    )(hidden, owners, slots)


def section_packet(core, key_weight, value_weight, hidden, taps):
    depth, features = key_weight.shape
    tok_rows, count = hidden.shape[0], taps.shape[0]
    total = depth + tok_rows + 4 * count
    parts = 4
    part = depth // parts

    def body(core_ref, key_ref, value_ref, hidden_ref, taps_ref, out_ref, terms_ref, sems):
        def weight_copy(source, i):
            span = pl.ds(i * part, part)
            return pltpu.make_async_copy(source.at[span], out_ref.at[span], sems.at[i])

        for mine, source in ((0, key_ref), (1, value_ref)):

            @pl.when(core_ref[0] == mine)
            def _(source=source):
                for i in range(parts):
                    weight_copy(source, i).start()

        rows_copy = pltpu.make_async_copy(hidden_ref, out_ref.at[pl.ds(depth, tok_rows)], sems.at[parts])
        rows_copy.start()
        taps_value = taps_ref[...]
        high = taps_value.astype(jnp.bfloat16).astype(jnp.float32)
        middle = (taps_value - high).astype(jnp.bfloat16).astype(jnp.float32)
        low = taps_value - high - middle
        terms = jnp.concatenate([high, middle, low, jnp.zeros_like(low)], axis=0)
        terms_ref[...] = terms.astype(jnp.bfloat16)
        taps_copy = pltpu.make_async_copy(
            terms_ref, out_ref.at[pl.ds(depth + tok_rows, 4 * count)], sems.at[parts + 1]
        )
        taps_copy.start()
        for i in range(parts):
            weight_copy(key_ref, i).wait()
        rows_copy.wait()
        taps_copy.wait()

    return pl.pallas_call(
        body,
        in_specs=[SMEM, ANY, ANY, ANY, VMEM],
        out_specs=ANY,
        out_shape=jax.ShapeDtypeStruct((total, features), jnp.bfloat16),
        scratch_shapes=[pltpu.VMEM((4 * count, features), jnp.bfloat16), pltpu.SemaphoreType.DMA((parts + 2,))],
        name="section_packet",
    )(core, key_weight, value_weight, hidden, taps)


def dense(place, own, sums, tail, packet, other_packet, depth, chunk, taps_count):
    features = packet.shape[1]
    rows = chunk + HALO

    def body(place_ref, own_ref, *refs):
        sums_refs, refs = refs[: len(sums)], refs[len(sums) :]
        tail_ref, packet_ref, other_ref, out_ref, product_ref, normed_ref = refs
        total = own_ref[...]
        for sums_ref in sums_refs:
            total = total + sums_ref[...].astype(jnp.float32)
        packed = total.astype(jnp.bfloat16)
        core = place_ref[1]
        product_ref[core] = jnp.dot(packed, packet_ref[:depth], preferred_element_type=jnp.float32)
        product_ref[1 - core] = jnp.dot(packed, other_ref[:depth], preferred_element_type=jnp.float32)

        def gate(at, states):
            states = states.astype(jnp.float32)
            keys = product_ref[0, pl.ds(at, HALO)]
            mean_states = jnp.mean(states * states, axis=-1, keepdims=True)
            mean_keys = jnp.mean(keys * keys, axis=-1, keepdims=True)
            affinity = jnp.sum(states * keys, axis=-1, keepdims=True)
            affinity = affinity * lax.rsqrt(mean_states + 1e-06) * lax.rsqrt(mean_keys + 1e-06)
            gated = jax.nn.sigmoid(affinity / math.sqrt(features)) * product_ref[1, pl.ds(at, HALO)]
            product_ref[1, pl.ds(at, HALO)] = gated
            return gated * lax.rsqrt(jnp.mean(gated * gated, axis=-1, keepdims=True) + 1e-06)

        normed_ref[:HALO] = jnp.where(place_ref[0] > 0, gate(0, tail_ref[:HALO]), 0.0)
        terms = packet_ref[depth + chunk :].astype(jnp.float32)
        taps = terms[:taps_count] + terms[taps_count : 2 * taps_count] + terms[2 * taps_count : 3 * taps_count]

        def step(i, carry):
            at = pl.multiple_of((i + 1) * HALO, HALO)
            before = pl.multiple_of(i * HALO, HALO)
            states = packet_ref[pl.ds(pl.multiple_of(depth + i * HALO, HALO), HALO)]
            normed = gate(at, states)
            normed_ref[pl.ds(at, HALO)] = normed
            window = jnp.concatenate([normed_ref[pl.ds(before, HALO)], normed], axis=0)
            convolved = taps[0:1] * normed
            for k in range(1, taps_count):
                start = HALO - k * CONV_DILATION
                convolved = convolved + taps[k : k + 1] * window[start : start + HALO]
            branch = convolved * jax.nn.sigmoid(convolved) + product_ref[1, pl.ds(at, HALO)]
            out_ref[pl.ds(before, HALO)] = (states.astype(jnp.float32) + branch).astype(jnp.bfloat16)
            return carry

        lax.fori_loop(0, chunk // HALO, step, 0)

    return pl.pallas_call(
        body,
        in_specs=[SMEM] + [VMEM] * (4 + len(sums)),
        out_specs=VMEM,
        out_shape=jax.ShapeDtypeStruct((chunk, features), jnp.bfloat16),
        scratch_shapes=[
            pltpu.VMEM((2, rows, features), jnp.float32),
            pltpu.VMEM((rows, features), jnp.float32),
        ],
        name="dense",
    )(place, own, *sums, tail, packet, other_packet)


def local(hidden, owner, slot, memory_table, key_weight, value_weight, conv_weight):
    bf16 = jnp.bfloat16
    tok_rows, head_count = owner.shape[1:]
    rows_dev, row_features = memory_table.shape[1:]
    x, y, core = (lax.axis_index(name) for name in TABLE)

    table = rotated(memory_table[0], "segment", 1)
    numbers, tail = edge_packet(hidden[0], owner[0].T, slot[0].T)
    numbers = rotated(numbers, "segment", 1)
    shards = NX * NY * NC
    sections = lax.axis_size("segment")
    tail = lax.ppermute(
        tail,
        TABLE + ("segment",),
        [
            (i * sections + s, (i + 1) * sections + (s + 1) % sections)
            for i in range(shards - 1)
            for s in range(sections)
        ],
    )
    packet = section_packet(
        core.astype(jnp.int32).reshape(1), key_weight[0], value_weight[0], hidden[0], conv_weight[0]
    )
    packet = rotated(packet, "segment", 1)
    other_packet = rotated(packet, "core", 1)

    copies = jnp.broadcast_to(table[None], (NY, rows_dev, row_features))
    own_rows = lax.all_to_all(copies, "y", split_axis=0, concat_axis=0, tiled=True)
    own_rows = own_rows.reshape(NY * rows_dev, row_features)
    other_rows = rotated(own_rows, "core", 1)

    head_numbers = tail[HALO:, 128 - HALO : 128].astype(jnp.int32)
    numbers = jnp.concatenate([head_numbers, numbers], axis=1)
    place = lax.broadcasted_iota(jnp.int32, (shards, 1), 0)
    ahead, swapped, far = place // (NY * NC), place // NY % NC, place % NY
    shard = (x + ahead) % NX * (NY * NC) + far * NC + (core ^ swapped)
    asked = jnp.full((shards, tok_rows + HALO), -1, jnp.int32)
    for h in range(head_count):
        asked = jnp.maximum(
            asked, jnp.where(numbers[h][None, :] == shard, numbers[head_count + h][None, :], -1)
        )
    asked = asked.reshape(NX, NY * NC, tok_rows + HALO)
    received = [asked[0]]
    for ahead in range(1, NX):
        received.append(rotated(asked[ahead], "x", ahead))
    asked = jnp.stack(received).transpose(0, 2, 1)
    pick_own, pick_other = pick_matrices(asked, rows_dev)

    rows = tok_rows + HALO
    rows = tok_rows + HALO
    own_part = jnp.dot(
        pick_own[1:].reshape((NX - 1) * rows, -1), own_rows, preferred_element_type=jnp.float32
    ).reshape(NX - 1, rows, -1)
    sums = []
    for back in (2, 1, 3):
        part = own_part[back - 1] + jnp.dot(pick_other[back], other_rows, preferred_element_type=jnp.float32)
        sums.append(rotated(part.astype(bf16), "x", -back))
    mine = jnp.dot(pick_own[0], own_rows, preferred_element_type=jnp.float32) + jnp.dot(
        pick_other[0], other_rows, preferred_element_type=jnp.float32
    )
    later = (x > 0) | (y > 0) | (core > 0)
    place = jnp.stack([later.astype(jnp.int32), core.astype(jnp.int32)])
    taps_count, depth = conv_weight.shape[1], key_weight.shape[1]
    return dense(place, mine, sums, tail, packet, other_packet, depth, tok_rows, taps_count)[None]


def solution(mesh):
    grid = Mesh(mesh.devices.reshape(NX, NY, NC, -1), TABLE + ("segment",))
    in_specs = (
        P("segment", TABLE, None),
        P("segment", TABLE, None),
        P("segment", TABLE, None),
        P("segment", TABLE, None),
        P("segment", None, None),
        P("segment", None, None),
        P("segment", None, None),
    )
    out_specs = P("segment", TABLE, None)

    return jax.shard_map(local, mesh=grid, in_specs=in_specs, out_specs=out_specs, check_vma=False)
```

```python
import math

import jax
import jax.numpy as jnp
from jax import lax
from jax.experimental import pallas as pl
from jax.experimental.pallas import tpu as pltpu
from jax.sharding import Mesh, PartitionSpec as P


CONV_DILATION = 3
NX, NY, NC = 4, 8, 2
HALO = 16
TABLE = ("x", "y", "core")


def rotated(value, axis, by):
    count = lax.axis_size(axis)
    return lax.ppermute(value, axis, [(i, (i + by) % count) for i in range(count)])


VMEM = pl.BlockSpec(memory_space=pltpu.VMEM)


def pick_matrices(asked, rows_dev):
    groups, rows, _ = asked.shape

    def body(asked_ref, own_ref, other_ref):
        lane = lax.broadcasted_iota(jnp.int32, (rows, rows_dev), 1)
        for group in range(groups):
            for swapped, out_ref in ((0, own_ref), (1, other_ref)):
                for far in range(NY):
                    column = swapped * NY + far
                    hit = asked_ref[group, :, column : column + 1] == lane
                    hit = hit.astype(jnp.float32).astype(jnp.bfloat16)
                    out_ref[group, :, far * rows_dev : (far + 1) * rows_dev] = hit

    shape = jax.ShapeDtypeStruct((groups, rows, NY * rows_dev), jnp.bfloat16)
    return pl.pallas_call(
        body,
        in_specs=[VMEM],
        out_specs=[VMEM, VMEM],
        out_shape=[shape, shape],
        name="pick_matrices",
    )(asked)


def rms_scale(values):
    return values * lax.rsqrt(jnp.mean(values * values, axis=-1, keepdims=True) + 1e-06)


def edge_packet(hidden, owners, slots):
    heads, tok_rows = owners.shape
    features = hidden.shape[1]

    def body(hidden_ref, owners_ref, slots_ref, numbers_ref, tail_ref):
        numbers_ref[:heads] = owners_ref[...]
        numbers_ref[heads:] = slots_ref[...]
        tail_ref[:HALO] = hidden_ref[...]
        last = numbers_ref[:, tok_rows - 128 :].astype(jnp.float32)
        tail_ref[HALO:, :128] = last.astype(jnp.bfloat16)
        tail_ref[HALO:, 128:] = jnp.zeros((2 * heads, features - 128), jnp.bfloat16)

    return pl.pallas_call(
        body,
        grid=(1,),
        in_specs=[
            pl.BlockSpec((HALO, features), lambda i: (tok_rows // HALO - 1, 0)),
            pl.BlockSpec((heads, tok_rows), lambda i: (0, 0)),
            pl.BlockSpec((heads, tok_rows), lambda i: (0, 0)),
        ],
        out_specs=[
            pl.BlockSpec((2 * heads, tok_rows), lambda i: (0, 0)),
            pl.BlockSpec((HALO + 2 * heads, features), lambda i: (0, 0)),
        ],
        out_shape=[
            jax.ShapeDtypeStruct((2 * heads, tok_rows), jnp.int32),
            jax.ShapeDtypeStruct((HALO + 2 * heads, features), jnp.bfloat16),
        ],
        name="edge_packet",
    )(hidden, owners, slots)


def local(hidden, owner, slot, memory_table, key_weight, value_weight, conv_weight):
    bf16 = jnp.bfloat16
    tok_rows, head_count = owner.shape[1:]
    features = hidden.shape[2]
    rows_dev, row_features = memory_table.shape[1:]
    x, y, core = (lax.axis_index(name) for name in TABLE)
    first = (x == 0) & (y == 0) & (core == 0)

    table = rotated(memory_table[0], "segment", 1)
    numbers, tail = edge_packet(hidden[0], owner[0].T, slot[0].T)
    numbers = rotated(numbers, "segment", 1)
    shards = NX * NY * NC
    sections = lax.axis_size("segment")
    tail = lax.ppermute(
        tail,
        TABLE + ("segment",),
        [
            (i * sections + s, (i + 1) * sections + (s + 1) % sections)
            for i in range(shards - 1)
            for s in range(sections)
        ],
    )
    states = rotated(hidden[0], "segment", 1)
    weight_one = jnp.where(core == 0, key_weight[0], value_weight[0])
    weight_one = rotated(weight_one, "segment", 1)
    weight_two = rotated(weight_one, "core", 1)
    taps = rotated(conv_weight[0], "segment", 1)

    copies = jnp.broadcast_to(table[None], (NY, rows_dev, row_features))
    own_rows = lax.all_to_all(copies, "y", split_axis=0, concat_axis=0, tiled=True)
    own_rows = own_rows.reshape(NY * rows_dev, row_features)
    other_rows = rotated(own_rows, "core", 1)

    head_numbers = tail[HALO:, 128 - HALO : 128].astype(jnp.int32)
    numbers = jnp.concatenate([head_numbers, numbers], axis=1)
    place = lax.broadcasted_iota(jnp.int32, (shards, 1), 0)
    ahead, swapped, far = place // (NY * NC), place // NY % NC, place % NY
    shard = (x + ahead) % NX * (NY * NC) + far * NC + (core ^ swapped)
    asked = jnp.full((shards, tok_rows + HALO), -1, jnp.int32)
    for h in range(head_count):
        asked = jnp.maximum(
            asked, jnp.where(numbers[h][None, :] == shard, numbers[head_count + h][None, :], -1)
        )
    asked = asked.reshape(NX, NY * NC, tok_rows + HALO)
    received = [asked[0]]
    for ahead in range(1, NX):
        received.append(rotated(asked[ahead], "x", ahead))
    asked = jnp.stack(received).transpose(0, 2, 1)
    pick_own, pick_other = pick_matrices(asked, rows_dev)

    rows = tok_rows + HALO
    pick_sent = pick_own[1:].reshape((NX - 1) * rows, -1)
    own_part = jnp.dot(pick_sent, own_rows, preferred_element_type=jnp.float32).reshape(NX - 1, rows, -1)
    sums = []
    for back in (2, 1, 3):
        part = own_part[back - 1] + jnp.dot(pick_other[back], other_rows, preferred_element_type=jnp.float32)
        sums.append(rotated(part.astype(bf16), "x", -back))
    total = jnp.dot(pick_own[0], own_rows, preferred_element_type=jnp.float32) + jnp.dot(
        pick_other[0], other_rows, preferred_element_type=jnp.float32
    )
    total = lax.optimization_barrier(total)
    key_here = jnp.where(core == 0, weight_one, weight_two)
    value_here = jnp.where(core == 0, weight_two, weight_one)
    key_here, value_here = lax.optimization_barrier((key_here, value_here))
    for part in sums:
        total = total + part.astype(jnp.float32)
    packed = total.astype(bf16)

    states_float = jnp.concatenate([tail[:HALO], states], axis=0).astype(jnp.float32)
    keys_out = jnp.dot(packed, key_here, preferred_element_type=jnp.float32)
    values_out = jnp.dot(packed, value_here, preferred_element_type=jnp.float32)
    affinity = jnp.sum(rms_scale(states_float) * rms_scale(keys_out), axis=-1, keepdims=True) / math.sqrt(features)
    gated = jax.nn.sigmoid(affinity) * values_out
    normed = rms_scale(gated)
    before = lax.broadcasted_iota(jnp.int32, (rows, 1), 0) < HALO
    normed = jnp.where(before & first, 0.0, normed)
    convolved = jnp.zeros((tok_rows, features), jnp.float32)
    for k in range(taps.shape[0]):
        start = HALO - k * CONV_DILATION
        convolved = convolved + taps[k] * normed[start : start + tok_rows]
    branch = jax.nn.silu(convolved) + gated[HALO:]
    return (states_float[HALO:] + branch).astype(bf16)[None]


def solution(mesh):
    grid = Mesh(mesh.devices.reshape(NX, NY, NC, -1), TABLE + ("segment",))
    in_specs = (
        P("segment", TABLE, None),
        P("segment", TABLE, None),
        P("segment", TABLE, None),
        P("segment", TABLE, None),
        P("segment", None, None),
        P("segment", None, None),
        P("segment", None, None),
    )
    out_specs = P("segment", TABLE, None)

    return jax.shard_map(local, mesh=grid, in_specs=in_specs, out_specs=out_specs, check_vma=False)
```

```python
import math

import jax
import jax.numpy as jnp
from jax import lax
from jax.experimental import pallas as pl
from jax.experimental.pallas import tpu as pltpu
from jax.sharding import Mesh, PartitionSpec as P


CONV_DILATION = 3
NX, NY, NC = 4, 8, 2
HALO = 16
TABLE = ("x", "y", "core")


def rotated(value, axis, by):
    count = lax.axis_size(axis)
    return lax.ppermute(value, axis, [(i, (i + by) % count) for i in range(count)])


VMEM = pl.BlockSpec(memory_space=pltpu.VMEM)


def pick_matrices(asked, rows_dev):
    groups, rows, _ = asked.shape

    def body(asked_ref, sent_ref, mine_ref, other_ref):
        lane = lax.broadcasted_iota(jnp.int32, (rows, rows_dev), 1)
        for group in range(groups):
            for column in range(NC * NY):
                hit = asked_ref[group, :, column : column + 1] == lane
                hit = hit.astype(jnp.float32).astype(jnp.bfloat16)
                at = column % NY * rows_dev
                if column >= NY:
                    other_ref[group, :, at : at + rows_dev] = hit
                elif group == 0:
                    mine_ref[:, at : at + rows_dev] = hit
                else:
                    sent_ref[(group - 1) * rows : group * rows, at : at + rows_dev] = hit

    wide = NY * rows_dev
    return pl.pallas_call(
        body,
        in_specs=[VMEM],
        out_specs=[VMEM] * 3,
        out_shape=[
            jax.ShapeDtypeStruct(((groups - 1) * rows, wide), jnp.bfloat16),
            jax.ShapeDtypeStruct((rows, wide), jnp.bfloat16),
            jax.ShapeDtypeStruct((groups, rows, wide), jnp.bfloat16),
        ],
        name="pick_matrices",
    )(asked)


def rms_scale(values):
    return values * lax.rsqrt(jnp.mean(values * values, axis=-1, keepdims=True) + 1e-06)


def edge_packet(hidden, owners, slots):
    heads, tok_rows = owners.shape
    features = hidden.shape[1]

    def body(hidden_ref, owners_ref, slots_ref, numbers_ref, tail_ref):
        numbers_ref[:heads] = owners_ref[...]
        numbers_ref[heads:] = slots_ref[...]
        tail_ref[:HALO] = hidden_ref[...]
        last = numbers_ref[:, tok_rows - 128 :].astype(jnp.float32)
        tail_ref[HALO:, :128] = last.astype(jnp.bfloat16)
        tail_ref[HALO:, 128:] = jnp.zeros((2 * heads, features - 128), jnp.bfloat16)

    return pl.pallas_call(
        body,
        grid=(1,),
        in_specs=[
            pl.BlockSpec((HALO, features), lambda i: (tok_rows // HALO - 1, 0)),
            pl.BlockSpec((heads, tok_rows), lambda i: (0, 0)),
            pl.BlockSpec((heads, tok_rows), lambda i: (0, 0)),
        ],
        out_specs=[
            pl.BlockSpec((2 * heads, tok_rows), lambda i: (0, 0)),
            pl.BlockSpec((HALO + 2 * heads, features), lambda i: (0, 0)),
        ],
        out_shape=[
            jax.ShapeDtypeStruct((2 * heads, tok_rows), jnp.int32),
            jax.ShapeDtypeStruct((HALO + 2 * heads, features), jnp.bfloat16),
        ],
        name="edge_packet",
    )(hidden, owners, slots)


def local(hidden, owner, slot, memory_table, key_weight, value_weight, conv_weight):
    bf16 = jnp.bfloat16
    tok_rows, head_count = owner.shape[1:]
    features = hidden.shape[2]
    rows_dev, row_features = memory_table.shape[1:]
    x, y, core = (lax.axis_index(name) for name in TABLE)
    first = (x == 0) & (y == 0) & (core == 0)

    table = rotated(memory_table[0], "segment", 1)
    numbers, tail = edge_packet(hidden[0], owner[0].T, slot[0].T)
    numbers = rotated(numbers, "segment", 1)
    shards = NX * NY * NC
    sections = lax.axis_size("segment")
    tail = lax.ppermute(
        tail,
        TABLE + ("segment",),
        [
            (i * sections + s, (i + 1) * sections + (s + 1) % sections)
            for i in range(shards - 1)
            for s in range(sections)
        ],
    )
    states = rotated(hidden[0], "segment", 1)
    weight_one = jnp.where(core == 0, key_weight[0], value_weight[0])
    weight_one = rotated(weight_one, "segment", 1)
    weight_two = rotated(weight_one, "core", 1)
    taps = rotated(conv_weight[0], "segment", 1)

    copies = jnp.broadcast_to(table[None], (NY, rows_dev, row_features))
    own_rows = lax.all_to_all(copies, "y", split_axis=0, concat_axis=0, tiled=True)
    own_rows = own_rows.reshape(NY * rows_dev, row_features)
    other_rows = rotated(own_rows, "core", 1)

    head_numbers = tail[HALO:, 128 - HALO : 128].astype(jnp.int32)
    numbers = jnp.concatenate([head_numbers, numbers], axis=1)
    place = lax.broadcasted_iota(jnp.int32, (shards, 1), 0)
    ahead, swapped, far = place // (NY * NC), place // NY % NC, place % NY
    shard = (x + ahead) % NX * (NY * NC) + far * NC + (core ^ swapped)
    asked = jnp.full((shards, tok_rows + HALO), -1, jnp.int32)
    for h in range(head_count):
        asked = jnp.maximum(
            asked, jnp.where(numbers[h][None, :] == shard, numbers[head_count + h][None, :], -1)
        )
    asked = asked.reshape(NX, NY * NC, tok_rows + HALO)
    received = [asked[0]]
    for ahead in range(1, NX):
        received.append(rotated(asked[ahead], "x", ahead))
    asked = jnp.stack(received).transpose(0, 2, 1)
    pick_sent, pick_mine, pick_other = pick_matrices(asked, rows_dev)

    rows = tok_rows + HALO
    own_part = jnp.dot(pick_sent, own_rows, preferred_element_type=jnp.float32).reshape(NX - 1, rows, -1)
    sums = []
    for back in (2, 1, 3):
        part = own_part[back - 1] + jnp.dot(pick_other[back], other_rows, preferred_element_type=jnp.float32)
        sums.append(rotated(part.astype(bf16), "x", -back))
    total = jnp.dot(pick_mine, own_rows, preferred_element_type=jnp.float32) + jnp.dot(
        pick_other[0], other_rows, preferred_element_type=jnp.float32
    )
    key_here = jnp.where(core == 0, weight_one, weight_two)
    value_here = jnp.where(core == 0, weight_two, weight_one)
    key_here, value_here, total, states = lax.optimization_barrier((key_here, value_here, total, states))
    for part in sums:
        total = total + part.astype(jnp.float32)
    packed = total.astype(bf16)

    states_float = jnp.concatenate([tail[:HALO], states], axis=0).astype(jnp.float32)
    keys_out = jnp.dot(packed, key_here, preferred_element_type=jnp.float32)
    values_out = jnp.dot(packed, value_here, preferred_element_type=jnp.float32)
    affinity = jnp.sum(rms_scale(states_float) * rms_scale(keys_out), axis=-1, keepdims=True) / math.sqrt(features)
    gated = jax.nn.sigmoid(affinity) * values_out
    normed = rms_scale(gated)
    before = lax.broadcasted_iota(jnp.int32, (rows, 1), 0) < HALO
    normed = jnp.where(before & first, 0.0, normed)
    convolved = jnp.zeros((tok_rows, features), jnp.float32)
    for k in range(taps.shape[0]):
        start = HALO - k * CONV_DILATION
        convolved = convolved + taps[k] * normed[start : start + tok_rows]
    branch = jax.nn.silu(convolved) + gated[HALO:]
    return (states_float[HALO:] + branch).astype(bf16)[None]


def solution(mesh):
    grid = Mesh(mesh.devices.reshape(NX, NY, NC, -1), TABLE + ("segment",))
    in_specs = (
        P("segment", TABLE, None),
        P("segment", TABLE, None),
        P("segment", TABLE, None),
        P("segment", TABLE, None),
        P("segment", None, None),
        P("segment", None, None),
        P("segment", None, None),
    )
    out_specs = P("segment", TABLE, None)

    return jax.shard_map(local, mesh=grid, in_specs=in_specs, out_specs=out_specs, check_vma=False)
```

```python
import math

import jax
import jax.numpy as jnp
from jax import lax
from jax.experimental import pallas as pl
from jax.experimental.pallas import tpu as pltpu
from jax.sharding import Mesh, PartitionSpec as P


CONV_DILATION = 3
NX, NY, NC = 4, 8, 2
HALO = 16
TABLE = ("x", "y", "core")
GROUPS = ((0, 1, 2, 3), (0, 3, 2, 1))


def rotated(value, axis, by):
    count = lax.axis_size(axis)
    return lax.ppermute(value, axis, [(i, (i + by) % count) for i in range(count)])


VMEM = pl.BlockSpec(memory_space=pltpu.VMEM)


def pick_matrices(asked, rows_dev):
    groups, rows, _ = asked.shape

    def body(asked_ref, sent_ref, mine_ref, other_ref):
        lane = lax.broadcasted_iota(jnp.int32, (rows, rows_dev), 1)
        for group in range(groups):
            for column in range(NC * NY):
                hit = asked_ref[group, :, column : column + 1] == lane
                hit = hit.astype(jnp.float32).astype(jnp.bfloat16)
                at = column % NY * rows_dev
                if column >= NY:
                    other_ref[group, :, at : at + rows_dev] = hit
                elif group == 0:
                    mine_ref[:, at : at + rows_dev] = hit
                else:
                    sent_ref[(group - 1) * rows : group * rows, at : at + rows_dev] = hit

    wide = NY * rows_dev
    return pl.pallas_call(
        body,
        in_specs=[VMEM],
        out_specs=[VMEM] * 3,
        out_shape=[
            jax.ShapeDtypeStruct(((groups - 1) * rows, wide), jnp.bfloat16),
            jax.ShapeDtypeStruct((rows, wide), jnp.bfloat16),
            jax.ShapeDtypeStruct((groups, rows, wide), jnp.bfloat16),
        ],
        name="pick_matrices",
    )(asked)


def along_x(value, steps):
    pairs = []
    for place in range(NX):
        for core in range(NC):
            pairs.append((place * NC + core, (place + steps[core]) % NX * NC + core))
    return lax.ppermute(value, ("x", "core"), pairs)


def rms_scale(values):
    return values * lax.rsqrt(jnp.mean(values * values, axis=-1, keepdims=True) + 1e-06)


def edge_packet(hidden, owners, slots):
    heads, tok_rows = owners.shape
    features = hidden.shape[1]

    def body(hidden_ref, owners_ref, slots_ref, numbers_ref, tail_ref):
        numbers_ref[:heads] = owners_ref[...]
        numbers_ref[heads:] = slots_ref[...]
        tail_ref[:HALO] = hidden_ref[...]
        last = numbers_ref[:, tok_rows - 128 :].astype(jnp.float32)
        tail_ref[HALO:, :128] = last.astype(jnp.bfloat16)
        tail_ref[HALO:, 128:] = jnp.zeros((2 * heads, features - 128), jnp.bfloat16)

    return pl.pallas_call(
        body,
        grid=(1,),
        in_specs=[
            pl.BlockSpec((HALO, features), lambda i: (tok_rows // HALO - 1, 0)),
            pl.BlockSpec((heads, tok_rows), lambda i: (0, 0)),
            pl.BlockSpec((heads, tok_rows), lambda i: (0, 0)),
        ],
        out_specs=[
            pl.BlockSpec((2 * heads, tok_rows), lambda i: (0, 0)),
            pl.BlockSpec((HALO + 2 * heads, features), lambda i: (0, 0)),
        ],
        out_shape=[
            jax.ShapeDtypeStruct((2 * heads, tok_rows), jnp.int32),
            jax.ShapeDtypeStruct((HALO + 2 * heads, features), jnp.bfloat16),
        ],
        name="edge_packet",
    )(hidden, owners, slots)


def local(hidden, owner, slot, memory_table, key_weight, value_weight, conv_weight):
    bf16 = jnp.bfloat16
    tok_rows, head_count = owner.shape[1:]
    features = hidden.shape[2]
    rows_dev, row_features = memory_table.shape[1:]
    x, y, core = (lax.axis_index(name) for name in TABLE)
    first = (x == 0) & (y == 0) & (core == 0)

    table = rotated(memory_table[0], "segment", 1)
    numbers, tail = edge_packet(hidden[0], owner[0].T, slot[0].T)
    numbers = rotated(numbers, "segment", 1)
    shards = NX * NY * NC
    sections = lax.axis_size("segment")
    tail = lax.ppermute(
        tail,
        TABLE + ("segment",),
        [
            (i * sections + s, (i + 1) * sections + (s + 1) % sections)
            for i in range(shards - 1)
            for s in range(sections)
        ],
    )
    states = rotated(hidden[0], "segment", 1)
    weight_one = jnp.where(core == 0, key_weight[0], value_weight[0])
    weight_one = rotated(weight_one, "segment", 1)
    weight_two = rotated(weight_one, "core", 1)
    taps = rotated(conv_weight[0], "segment", 1)

    copies = jnp.broadcast_to(table[None], (NY, rows_dev, row_features))
    own_rows = lax.all_to_all(copies, "y", split_axis=0, concat_axis=0, tiled=True)
    own_rows = own_rows.reshape(NY * rows_dev, row_features)
    other_rows = rotated(own_rows, "core", 1)

    head_numbers = tail[HALO:, 128 - HALO : 128].astype(jnp.int32)
    numbers = jnp.concatenate([head_numbers, numbers], axis=1)
    place = lax.broadcasted_iota(jnp.int32, (shards, 1), 0)
    group, swapped, far = place // (NY * NC), place // NY % NC, place % NY
    ahead = jnp.where(group % 2 == 1, (group + 2 * core) % NX, group)
    shard = (x + ahead) % NX * (NY * NC) + far * NC + (core ^ swapped)
    asked = jnp.full((shards, tok_rows + HALO), -1, jnp.int32)
    for h in range(head_count):
        asked = jnp.maximum(
            asked, jnp.where(numbers[h][None, :] == shard, numbers[head_count + h][None, :], -1)
        )
    asked = asked.reshape(NX, NY * NC, tok_rows + HALO)
    received = [asked[0]]
    for group in range(1, NX):
        received.append(along_x(asked[group], (GROUPS[0][group], GROUPS[1][group])))
    asked = jnp.stack(received).transpose(0, 2, 1)
    pick_sent, pick_mine, pick_other = pick_matrices(asked, rows_dev)

    rows = tok_rows + HALO
    own_part = jnp.dot(pick_sent, own_rows, preferred_element_type=jnp.float32).reshape(NX - 1, rows, -1)
    sums = []
    for back in (2, 1, 3):
        part = own_part[back - 1] + jnp.dot(pick_other[back], other_rows, preferred_element_type=jnp.float32)
        sums.append(along_x(part.astype(bf16), (-GROUPS[0][back], -GROUPS[1][back])))
    total = jnp.dot(pick_mine, own_rows, preferred_element_type=jnp.float32) + jnp.dot(
        pick_other[0], other_rows, preferred_element_type=jnp.float32
    )
    key_here = jnp.where(core == 0, weight_one, weight_two)
    value_here = jnp.where(core == 0, weight_two, weight_one)
    key_here, value_here, total, states = lax.optimization_barrier((key_here, value_here, total, states))
    total = lax.optimization_barrier(total + sums[0].astype(jnp.float32) + sums[1].astype(jnp.float32))
    packed = (total + sums[2].astype(jnp.float32)).astype(bf16)

    states_float = jnp.concatenate([tail[:HALO], states], axis=0).astype(jnp.float32)
    keys_out = jnp.dot(packed, key_here, preferred_element_type=jnp.float32)
    values_out = jnp.dot(packed, value_here, preferred_element_type=jnp.float32)
    affinity = jnp.sum(rms_scale(states_float) * rms_scale(keys_out), axis=-1, keepdims=True) / math.sqrt(features)
    gated = jax.nn.sigmoid(affinity) * values_out
    normed = rms_scale(gated)
    before = lax.broadcasted_iota(jnp.int32, (rows, 1), 0) < HALO
    normed = jnp.where(before & first, 0.0, normed)
    convolved = jnp.zeros((tok_rows, features), jnp.float32)
    for k in range(taps.shape[0]):
        start = HALO - k * CONV_DILATION
        convolved = convolved + taps[k] * normed[start : start + tok_rows]
    branch = jax.nn.silu(convolved) + gated[HALO:]
    return (states_float[HALO:] + branch).astype(bf16)[None]


def solution(mesh):
    grid = Mesh(mesh.devices.reshape(NX, NY, NC, -1), TABLE + ("segment",))
    in_specs = (
        P("segment", TABLE, None),
        P("segment", TABLE, None),
        P("segment", TABLE, None),
        P("segment", TABLE, None),
        P("segment", None, None),
        P("segment", None, None),
        P("segment", None, None),
    )
    out_specs = P("segment", TABLE, None)

    return jax.shard_map(local, mesh=grid, in_specs=in_specs, out_specs=out_specs, check_vma=False)
```

```python
import math

import jax
import jax.numpy as jnp
from jax import lax
from jax.experimental import pallas as pl
from jax.experimental.pallas import tpu as pltpu
from jax.sharding import Mesh, PartitionSpec as P


CONV_DILATION = 3
NX, NY, NC = 4, 8, 2
HALO = 16
TABLE = ("x", "y", "core")
GROUPS = ((0, 1, 2, 3), (0, 3, 2, 1))


def rotated(value, axis, by):
    count = lax.axis_size(axis)
    return lax.ppermute(value, axis, [(i, (i + by) % count) for i in range(count)])


VMEM = pl.BlockSpec(memory_space=pltpu.VMEM)


def pick_matrices(asked, rows_dev):
    groups, rows, _ = asked.shape

    def body(asked_ref, sent_ref, mine_ref, other_ref):
        lane = lax.broadcasted_iota(jnp.int32, (rows, rows_dev), 1)
        for group in range(groups):
            for column in range(NC * NY):
                hit = asked_ref[group, :, column : column + 1] == lane
                hit = hit.astype(jnp.float32).astype(jnp.bfloat16)
                at = column % NY * rows_dev
                if column >= NY:
                    other_ref[group, :, at : at + rows_dev] = hit
                elif group == 0:
                    mine_ref[:, at : at + rows_dev] = hit
                else:
                    sent_ref[(group - 1) * rows : group * rows, at : at + rows_dev] = hit

    wide = NY * rows_dev
    return pl.pallas_call(
        body,
        in_specs=[VMEM],
        out_specs=[VMEM] * 3,
        out_shape=[
            jax.ShapeDtypeStruct(((groups - 1) * rows, wide), jnp.bfloat16),
            jax.ShapeDtypeStruct((rows, wide), jnp.bfloat16),
            jax.ShapeDtypeStruct((groups, rows, wide), jnp.bfloat16),
        ],
        name="pick_matrices",
    )(asked)


def along_x(value, steps):
    pairs = []
    for place in range(NX):
        for core in range(NC):
            pairs.append((place * NC + core, (place + steps[core]) % NX * NC + core))
    return lax.ppermute(value, ("x", "core"), pairs)


def rms_scale(values):
    return values * lax.rsqrt(jnp.mean(values * values, axis=-1, keepdims=True) + 1e-06)


def edge_packet(hidden, owners, slots):
    heads, tok_rows = owners.shape
    features = hidden.shape[1]

    def body(hidden_ref, owners_ref, slots_ref, numbers_ref, tail_ref):
        numbers_ref[:heads] = owners_ref[...]
        numbers_ref[heads:] = slots_ref[...]
        tail_ref[:HALO] = hidden_ref[...]
        last = numbers_ref[:, tok_rows - 128 :].astype(jnp.float32)
        tail_ref[HALO:, :128] = last.astype(jnp.bfloat16)
        tail_ref[HALO:, 128:] = jnp.zeros((2 * heads, features - 128), jnp.bfloat16)

    return pl.pallas_call(
        body,
        grid=(1,),
        in_specs=[
            pl.BlockSpec((HALO, features), lambda i: (tok_rows // HALO - 1, 0)),
            pl.BlockSpec((heads, tok_rows), lambda i: (0, 0)),
            pl.BlockSpec((heads, tok_rows), lambda i: (0, 0)),
        ],
        out_specs=[
            pl.BlockSpec((2 * heads, tok_rows), lambda i: (0, 0)),
            pl.BlockSpec((HALO + 2 * heads, features), lambda i: (0, 0)),
        ],
        out_shape=[
            jax.ShapeDtypeStruct((2 * heads, tok_rows), jnp.int32),
            jax.ShapeDtypeStruct((HALO + 2 * heads, features), jnp.bfloat16),
        ],
        name="edge_packet",
    )(hidden, owners, slots)


def local(hidden, owner, slot, memory_table, key_weight, value_weight, conv_weight):
    bf16 = jnp.bfloat16
    tok_rows, head_count = owner.shape[1:]
    features = hidden.shape[2]
    rows_dev, row_features = memory_table.shape[1:]
    x, y, core = (lax.axis_index(name) for name in TABLE)
    first = (x == 0) & (y == 0) & (core == 0)

    table = rotated(memory_table[0], "segment", 1)
    numbers, tail = edge_packet(hidden[0], owner[0].T, slot[0].T)
    numbers = rotated(numbers, "segment", 1)
    shards = NX * NY * NC
    sections = lax.axis_size("segment")
    tail = lax.ppermute(
        tail,
        TABLE + ("segment",),
        [
            (i * sections + s, (i + 1) * sections + (s + 1) % sections)
            for i in range(shards - 1)
            for s in range(sections)
        ],
    )
    states = rotated(hidden[0], "segment", 1)
    weight_one = jnp.where(core == 0, key_weight[0], value_weight[0])
    weight_one = rotated(weight_one, "segment", 1)
    taps = rotated(conv_weight[0], "segment", 1)

    copies = jnp.broadcast_to(table[None], (NY, rows_dev, row_features))
    own_rows = lax.all_to_all(copies, "y", split_axis=0, concat_axis=0, tiled=True)
    own_rows = own_rows.reshape(NY * rows_dev, row_features)
    other_rows = rotated(own_rows, "core", 1)

    head_numbers = tail[HALO:, 128 - HALO : 128].astype(jnp.int32)
    numbers = jnp.concatenate([head_numbers, numbers], axis=1)
    place = lax.broadcasted_iota(jnp.int32, (shards, 1), 0)
    group, swapped, far = place // (NY * NC), place // NY % NC, place % NY
    ahead = jnp.where(group % 2 == 1, (group + 2 * core) % NX, group)
    shard = (x + ahead) % NX * (NY * NC) + far * NC + (core ^ swapped)
    asked = jnp.full((shards, tok_rows + HALO), -1, jnp.int32)
    for h in range(head_count):
        asked = jnp.maximum(
            asked, jnp.where(numbers[h][None, :] == shard, numbers[head_count + h][None, :], -1)
        )
    asked = asked.reshape(NX, NY * NC, tok_rows + HALO)
    received = [asked[0]]
    for group in range(1, NX):
        received.append(along_x(asked[group], (GROUPS[0][group], GROUPS[1][group])))
    asked = jnp.stack(received).transpose(0, 2, 1)
    pick_sent, pick_mine, pick_other = pick_matrices(asked, rows_dev)
    pick_sent, weight_one = lax.optimization_barrier((pick_sent, weight_one))
    weight_two = rotated(weight_one, "core", 1)

    rows = tok_rows + HALO
    own_part = jnp.dot(pick_sent, own_rows, preferred_element_type=jnp.float32).reshape(NX - 1, rows, -1)
    sums = []
    for back in (2, 1, 3):
        part = own_part[back - 1] + jnp.dot(pick_other[back], other_rows, preferred_element_type=jnp.float32)
        sums.append(along_x(part.astype(bf16), (-GROUPS[0][back], -GROUPS[1][back])))
    total = jnp.dot(pick_mine, own_rows, preferred_element_type=jnp.float32) + jnp.dot(
        pick_other[0], other_rows, preferred_element_type=jnp.float32
    )
    key_here = jnp.where(core == 0, weight_one, weight_two)
    value_here = jnp.where(core == 0, weight_two, weight_one)
    key_here, value_here, total, states = lax.optimization_barrier((key_here, value_here, total, states))
    for part in sums:
        total = total + part.astype(jnp.float32)
    packed = total.astype(bf16)

    states_float = jnp.concatenate([tail[:HALO], states], axis=0).astype(jnp.float32)
    keys_out = jnp.dot(packed, key_here, preferred_element_type=jnp.float32)
    values_out = jnp.dot(packed, value_here, preferred_element_type=jnp.float32)
    affinity = jnp.sum(rms_scale(states_float) * rms_scale(keys_out), axis=-1, keepdims=True) / math.sqrt(features)
    gated = jax.nn.sigmoid(affinity) * values_out
    normed = rms_scale(gated)
    before = lax.broadcasted_iota(jnp.int32, (rows, 1), 0) < HALO
    normed = jnp.where(before & first, 0.0, normed)
    convolved = jnp.zeros((tok_rows, features), jnp.float32)
    for k in range(taps.shape[0]):
        start = HALO - k * CONV_DILATION
        convolved = convolved + taps[k] * normed[start : start + tok_rows]
    branch = jax.nn.silu(convolved) + gated[HALO:]
    return (states_float[HALO:] + branch).astype(bf16)[None]


def solution(mesh):
    grid = Mesh(mesh.devices.reshape(NX, NY, NC, -1), TABLE + ("segment",))
    in_specs = (
        P("segment", TABLE, None),
        P("segment", TABLE, None),
        P("segment", TABLE, None),
        P("segment", TABLE, None),
        P("segment", None, None),
        P("segment", None, None),
        P("segment", None, None),
    )
    out_specs = P("segment", TABLE, None)

    return jax.shard_map(local, mesh=grid, in_specs=in_specs, out_specs=out_specs, check_vma=False)
```
